32 devices in a mesh: vocab: 8 (over z, y), section: 4 (over x, core).
Axes of the slice: x: 2, y: 2, z: 4, core: 2. Of those that a mesh axis runs over, the one named last changes fastest.
Arguments:
- hidden: bfloat16 [512, 8192], P('section', 'vocab'), may hold values from -2 to 2
- targets: int32 [512], replicated, may hold values from 0 to 12287
- out_weight: bfloat16 [12288, 8192], P(('vocab', 'section')), may hold values from -2 to 2
Outputs:
- token_loss: float32 [512], replicated
- weight_grad: bfloat16 [12288, 8192], P(('vocab', 'section'))
- sent_grad: bfloat16 [512, 8192], P('section', 'vocab')
The draws below stay inside these ranges and needn't reach their ends.
All inputs are finite; a program needn't handle non-finite values.
Results may differ from the reference program's by a relative error of at most 0.0033.
Values may be sent and summed in bfloat16 or wider, within the bound.
No kernel may reach another device: no remote copies, remote signals or barrier semaphores. Data moves between devices by JAX's collectives and lax.ppermute only.
A program may use at most 128 MiB of HBM per device.

```python
import math
import jax
import jax.numpy as jnp
import numpy as np

D = 8192
TOKENS = 512
VOCAB = 12288
N_SECTION = 4


def weight_row(key, index):
    scale = 13.6 / D ** 0.5
    limit = min(4.0 * scale, 2.0)
    row = scale * jax.random.normal(jax.random.fold_in(key, index), (D,), jnp.float32)
    return jnp.clip(row, -limit, limit)


def weight_rows(key, indices):
    base = jax.random.fold_in(key, 11)
    return jax.vmap(lambda index: weight_row(base, index))(indices)


def draw_out_weight(key, part):
    full = weight_rows(key, jnp.arange(VOCAB, dtype=jnp.int32))
    return full.astype(jnp.bfloat16)


def draw_hidden(key, part):
    inner = jax.random.fold_in(key, 23)
    states = 0.25 * jax.random.normal(inner, (TOKENS, D), jnp.float32)
    return jnp.clip(states, -2.0, 2.0).astype(jnp.bfloat16)


def plant(values, own_key, low, top_value):
    longest = values.shape.index(max(values.shape))
    spots = []
    for shift in (0, 1):
        where = [jax.random.randint(jax.random.fold_in(own_key, axis), (), 0, length) for axis, length in enumerate(values.shape)]
        where[longest] = (where[longest] + shift) % values.shape[longest]
        spots.append(tuple(where))
    return values.at[spots[0]].set(low).at[spots[1]].set(top_value)


def rank_table(amount, skew):
    portions = [(1 << 20) // math.isqrt(grade ** skew) + 1 for grade in range(1, amount + 1)]
    scale = 1 + sum(portions) // (1 << 30)
    return np.cumsum(np.array([max(1, weight // scale) for weight in portions]))


def skewed_ids(rng, dims, number_of, lean):
    grid = rank_table(number_of, lean)
    pick = jax.random.randint(jax.random.fold_in(rng, 1), dims, 0, int(grid[number_of - 1]))
    grade = jnp.searchsorted(jnp.asarray(grid, jnp.int32), pick, side="right")
    return jax.random.permutation(jax.random.fold_in(rng, 2), number_of)[grade].astype(jnp.int32)


def setup_inputs(seed: int = 0) -> dict:
    keys = jax.random.split(jax.random.key(seed), 4)
    return {
        "hidden": draw_hidden(jax.random.fold_in(keys[3], 71), 0),
        "targets": plant(skewed_ids(keys[1], (TOKENS,), VOCAB, 2), jax.random.fold_in(keys[1], 3), 0, VOCAB - 1).astype(jnp.int32),
        "out_weight": draw_out_weight(jax.random.fold_in(keys[3], 71), 0),
    }


def reference(hidden, targets, out_weight):
    logits = jnp.dot(hidden, out_weight.T, preferred_element_type=jnp.float32)
    top = jnp.max(logits, axis=1)
    picked = targets[:, None] == jnp.arange(VOCAB, dtype=jnp.int32)[None, :]
    target_logit = jnp.sum(jnp.where(picked, logits, jnp.float32(0.0)), axis=1)
    expd = jnp.exp(logits - top[:, None])
    total = jnp.sum(expd, axis=1)
    token_loss = top + jnp.log(total) - target_logit
    dlogits = (expd / total[:, None] - picked.astype(jnp.float32)).astype(jnp.bfloat16)
    weight_grad = jnp.dot(dlogits.T, hidden, preferred_element_type=jnp.float32).astype(jnp.bfloat16)
    hidden_grad = jnp.dot(dlogits, out_weight, preferred_element_type=jnp.float32)
    sent_grad = jnp.roll(hidden_grad, -(TOKENS // N_SECTION), axis=0).astype(jnp.bfloat16)
    return token_loss, weight_grad, sent_grad
```

```python
import functools

import jax
import jax.numpy as jnp
from jax import lax
from jax.experimental import pallas as pl
from jax.experimental.pallas import tpu as pltpu
from jax.sharding import PartitionSpec as P

AXES = ("vocab", "section")
CORES = 2
SCALE = 8192.0


class Grid:
    def __init__(self, n_vocab, n_section):
        self.x = n_section // CORES
        self.y = self.x if n_vocab % self.x == 0 else 1
        self.z = n_vocab // self.y
        self.colours = self.x == self.y

    def devices(self):
        for z in range(self.z):
            for y in range(self.y):
                for x in range(self.x):
                    for c in range(CORES):
                        yield z, y, x, c

    def index(self, z, y, x, c):
        return (z * self.y + y) * self.x * CORES + x * CORES + c

    def permute(self, value, to):
        pairs = [(self.index(*d), self.index(*to(*d))) for d in self.devices()]
        return lax.ppermute(value, AXES, pairs)

    def along_z(self, value, k):
        return self.permute(value, lambda z, y, x, c: ((z + k) % self.z, y, x, c))

    def along_core(self, value):
        return self.permute(value, lambda z, y, x, c: (z, y, x, (c + 1) % CORES))

    def x_first(self, c):
        return c == 0 or not self.colours

    def along_first(self, value, k):
        def to(z, y, x, c):
            if self.x_first(c):
                return z, y, (x + k) % self.x, c
            return z, (y + k) % self.y, x, c

        return self.permute(value, to)

    def along_second(self, value, k):
        def to(z, y, x, c):
            if self.x_first(c):
                return z, (y + k) % self.y, x, c
            return z, y, (x + k) % self.x, c

        return self.permute(value, to)


def gather_kernel(n_first, first, table, *refs):
    if first:
        *blocks, w, whole, logits = refs
    else:
        *blocks, w, _, before, whole, logits = refs
    rows, columns = blocks[0].shape[-2:]
    entry = 1
    for ref in blocks:
        for b in range(ref.shape[0]):
            place, feature = table[entry], table[entry + 1]
            entry += 2
            at_row = pl.ds(pl.multiple_of(place * rows, rows), rows)
            at_column = pl.ds(pl.multiple_of(feature * columns, columns), columns)
            whole[at_row, at_column] = ref[b]
    part = lax.dot_general(
        w[...], whole[...], (((1,), (1,)), ((), ())), preferred_element_type=jnp.float32
    )
    logits[...] = part if first else before[...] + part


def gather_step(table, blocks, out_weight, carried, tokens, width):
    vocab, features = out_weight.shape
    full = lambda v: pl.BlockSpec(v.shape, lambda i, t: (0,) * v.ndim)
    strip = lambda n: pl.BlockSpec((n, width), lambda i, t: (0, t[0]))
    first = carried is None
    operands = [*blocks, out_weight]
    in_specs = [*(full(b) for b in blocks), strip(vocab)]
    aliases = {}
    if not first:
        operands += list(carried)
        in_specs += [pl.BlockSpec(memory_space=pl.ANY), full(carried[1])]
        aliases = {len(operands) - 1: 0, len(operands): 1}
    return pl.pallas_call(
        functools.partial(gather_kernel, None, first),
        grid_spec=pltpu.PrefetchScalarGridSpec(
            num_scalar_prefetch=1,
            grid=(1,),
            in_specs=in_specs,
            out_specs=[strip(tokens), pl.BlockSpec((vocab, tokens), lambda i, t: (0, 0))],
        ),
        out_shape=[
            jax.ShapeDtypeStruct((tokens, features), jnp.bfloat16),
            jax.ShapeDtypeStruct((vocab, tokens), jnp.float32),
        ],
        input_output_aliases=aliases,
        cost_estimate=pl.CostEstimate(
            flops=2 * vocab * tokens * width,
            bytes_accessed=2 * width * (vocab + 2 * tokens),
            transcendentals=0,
        ),
        name="gather_step",
    )(table, *operands)


def scatter_kernel(grid, rows, table, dlogits, w, keep, send):
    colour = table[1]
    columns = keep.shape[-1]
    for dy in range(grid.y):
        feature = table[2 + dy]
        block = w[:, pl.ds(pl.multiple_of(feature * columns, columns), columns)]
        part = SCALE * lax.dot_general(
            dlogits[...], block, (((0,), (0,)), ((), ())), preferred_element_type=jnp.float32
        )
        for dx in range(grid.x):
            x_first, y_first = dy * grid.x + dx, dx * grid.y + dy
            if grid.colours:
                own = jnp.where(colour == 0, x_first, y_first)
                other = jnp.where(colour == 0, y_first, x_first)
            else:
                own = other = x_first
            keep[own] = part[dx * rows : (dx + 1) * rows]
            at = (grid.x + dx) * rows
            send[other] = part[at : at + rows]


def scatter_step(grid, table, dlogits, out_weight, rows, width):
    vocab, tokens = dlogits.shape
    columns = width // grid.y
    shape = (grid.x * grid.y, rows, columns)
    whole = pl.BlockSpec(shape, lambda i, t: (0, 0, 0))
    return pl.pallas_call(
        functools.partial(scatter_kernel, grid, rows),
        grid_spec=pltpu.PrefetchScalarGridSpec(
            num_scalar_prefetch=1,
            grid=(1,),
            in_specs=[
                pl.BlockSpec((vocab, tokens), lambda i, t: (0, 0)),
                pl.BlockSpec((vocab, width), lambda i, t: (0, t[0])),
            ],
            out_specs=[whole, whole],
        ),
        out_shape=[jax.ShapeDtypeStruct(shape, jnp.float32)] * 2,
        cost_estimate=pl.CostEstimate(
            flops=2 * vocab * tokens * width,
            bytes_accessed=2 * vocab * (width + tokens) + 4 * tokens * width,
            transcendentals=0,
        ),
        name="scatter_step",
    )(table, dlogits, out_weight)


def on_device(grid, hidden, targets, out_weight):
    rows, columns = hidden.shape
    vocab = out_weight.shape[0]
    tokens = targets.shape[0]
    sections = grid.x * CORES
    width = grid.y * columns
    n_vocab = grid.z * grid.y
    v, s = lax.axis_index("vocab"), lax.axis_index("section")
    z, y = v // grid.y, v % grid.y
    x, c = s // CORES, s % CORES

    place = jnp.arange(sections, dtype=jnp.int32)
    ends = (x + place % grid.x) % grid.x * CORES + (c + place // grid.x) % CORES
    group = (ends + 1) % sections
    stands = group[:, None] == jnp.arange(sections, dtype=jnp.int32)[None, :]

    def to_places(value):
        parts = value.reshape(sections, 1, rows)
        return jnp.sum(jnp.where(stands.T[:, :, None], parts, 0), axis=0).reshape(tokens)

    def to_groups(value):
        parts = value.reshape(sections, 1, rows)
        return jnp.sum(jnp.where(stands[:, :, None], parts, 0), axis=0).reshape(tokens)

    per_side = grid.x * grid.y
    n = jnp.arange(CORES * per_side, dtype=jnp.int32)
    source_core = (c + n // per_side) % CORES
    rest = n % per_side
    if grid.colours:
        k_second, k_first = rest // grid.x, rest % grid.x
        dx = jnp.where(source_core == 0, k_first, k_second)
        dy = jnp.where(source_core == 0, k_second, k_first)
    else:
        dy, dx = rest // grid.x, rest % grid.x
    ends_at = ((x - dx) % grid.x * CORES + source_core - 1) % sections
    lies = (ends_at % CORES - c) % CORES * grid.x + (ends_at // CORES - x) % grid.x
    feature = (y - dy) % grid.y
    blocks_at = jnp.stack([lies, feature], axis=1).reshape(-1)

    at_z = [hidden] + [grid.along_z(hidden, k) for k in range(1, grid.z)]
    carried = None
    for k in range(grid.z):
        own = [at_z[k]] + [grid.along_first(at_z[k], j) for j in range(1, grid.x)]
        own = jnp.stack(own)
        mine = [own] + [grid.along_second(own, j) for j in range(1, grid.y)]
        theirs = [grid.along_core(m) for m in mine]
        table = jnp.concatenate([((z - k) % grid.z)[None].astype(jnp.int32), blocks_at])
        carried = gather_step(table, mine + theirs, out_weight, carried, tokens, width)
    whole, logits = carried

    wanted = to_places(targets) - (v * sections + s) * vocab
    picked = wanted[None, :] == jnp.arange(vocab, dtype=jnp.int32)[:, None]
    local_hit = jnp.sum(jnp.where(picked, logits, jnp.float32(0.0)), axis=0)
    local_top = jnp.max(logits, axis=0)
    local_sum = jnp.sum(jnp.exp(logits - local_top[None, :]), axis=0)
    local = jnp.stack([to_groups(local_top + jnp.log(local_sum)), to_groups(local_hit)])
    world = n_vocab * sections
    seen = lax.all_to_all(jnp.broadcast_to(local[None], (world, 2, tokens)), AXES, 0, 0)
    top = jnp.max(seen[:, 0], axis=0)
    log_total = top + jnp.log(jnp.sum(jnp.exp(seen[:, 0] - top[None]), axis=0))
    token_loss = log_total - jnp.sum(seen[:, 1], axis=0)
    probs = jnp.exp(logits - to_places(log_total)[None, :])
    dlogits = (probs - picked.astype(jnp.float32)).astype(jnp.bfloat16)

    half = jnp.float16
    f32 = jnp.float32
    total = None
    for k in [*range(1, grid.z), 0]:
        features = (y + jnp.arange(grid.y, dtype=jnp.int32)) % grid.y
        head = jnp.stack([(z + k) % grid.z, c]).astype(jnp.int32)
        keep, send = scatter_step(
            grid, jnp.concatenate([head, features]), dlogits, out_weight, rows, width
        )
        keep = keep + grid.along_core(send.astype(half)).astype(f32)
        keep = keep.reshape(grid.y, grid.x, rows, columns)
        got = [grid.along_second(keep[j].astype(half), j) for j in range(1, grid.y)]
        row = sum((g.astype(f32) for g in got), keep[0])
        got = [grid.along_first(row[j].astype(half), j) for j in range(1, grid.x)]
        part = sum((g.astype(f32) for g in got), row[0])
        if k:
            part = grid.along_z(part.astype(half), k).astype(f32)
        total = part if total is None else total + part
    sent_grad = (total * f32(1.0 / SCALE)).astype(jnp.bfloat16)

    weight_grad = jnp.dot(dlogits, whole, preferred_element_type=jnp.float32).astype(jnp.bfloat16)
    return (token_loss, weight_grad, sent_grad)


def solution(mesh):
    grid = Grid(mesh.shape["vocab"], mesh.shape["section"])
    in_specs = (P("section", "vocab"), P(), P(AXES, None))
    out_specs = (P(), P(AXES, None), P("section", "vocab"))
    return jax.shard_map(
        functools.partial(on_device, grid),
        mesh=mesh,
        in_specs=in_specs,
        out_specs=out_specs,
        check_vma=False,
    )
```
